32 devices in a mesh: groups: 2 (over x), gx: 16 (over z, y, core).
Axes of the slice: x: 2, y: 2, z: 4, core: 2. Of those that a mesh axis runs over, the one named last changes fastest.
Arguments:
- volume: bfloat16 [32, 64, 16, 256], P(None, ('groups', 'gx')), parts along dimension 1, may hold values from -6 to 6
- weight_two: bfloat16 [32, 32, 3, 3, 3], replicated, may hold values from -0.21875 to 0.21875
- weight_three: bfloat16 [64, 32, 3, 3, 3], replicated, may hold values from -0.21875 to 0.21875
- cotangent: bfloat16 [64, 32, 8, 128], P(None, ('groups', 'gx')), parts along dimension 1, may hold values from -6 to 6
Outputs:
- features_three: bfloat16 [64, 32, 8, 128], P(None, ('groups', 'gx')), parts along dimension 1
- grad_three: float32 [128, 32, 3, 3, 3], P(('groups', 'gx')), parts along dimension 0
- grad_two: float32 [64, 32, 3, 3, 3], P('groups'), parts along dimension 0
- grad_volume: bfloat16 [32, 64, 16, 256], P(None, ('groups', 'gx')), parts along dimension 1
The draws below stay inside these ranges and needn't reach their ends.
There are 2 independent parts, one for each index of `groups`. The reference program is written for one: setup_inputs(seed, part) draws one part's arguments, and reference() takes and returns one part's arrays. A program takes and returns all parts, laid end to end along the dimension named above; an argument that names none is the same for every part. Nothing has to cross between parts.
All inputs are finite; a program needn't handle non-finite values.
Results may differ from the reference program's by a relative error of at most 0.012.
Values may be sent and summed in bfloat16 or wider, within the bound.
A program may use at most 128 MiB of HBM per device.

```python
import jax
import jax.numpy as jnp
from jax import lax

CHANNELS = 32
FILTERS = 64
HEIGHT = 16
WIDTH = 256
DEPTH = 32
DEPTH_HALF = 16
HEIGHT_HALF = 8
WIDTH_HALF = 128


def spiked(array, stream_key, source, target, blocks, factor):
    def block_of(position):
        return (jnp.arange(array.shape[position]) // (array.shape[position] // blocks)).reshape((-1,) + (1,) * (array.ndim - 1 - position))

    first = jax.random.permutation(stream_key, blocks)[block_of(target)]
    far = (block_of(target) + blocks // 2) % blocks
    return jnp.where((block_of(source) == first) | (block_of(source) == far), factor * array, array)


def block_levels(rng, shape, shards, least, largest):
    factor_of, own = 1.0, jax.random.fold_in(rng, 6)
    for dim, shards_of in shards:
        steps = jnp.exp(jax.random.uniform(jax.random.fold_in(own, dim), (shards_of,), jnp.float32, least / len(shards), largest / len(shards)))
        factor_of = factor_of * jnp.repeat(steps, shape[dim] // shards_of).reshape([-1 if axis == dim else 1 for axis in range(len(shape))])
    return factor_of


def noise(rng, extent, deviation, limit, pieces=(), held_as=jnp.bfloat16):
    values = jax.random.normal(rng, extent, jnp.float32) * deviation
    if len(pieces) > 0:
        values = block_levels(rng, extent, pieces, -0.22, 0.18) * values
    return jnp.clip(values, min=-limit, max=limit).astype(held_as)


def gaussian_with(stream_key, dims, scale, bound, shards, heavy, kind=jnp.bfloat16):
    values = scale * jax.random.normal(stream_key, dims, jnp.float32)
    if shards:
        values = values * block_levels(stream_key, dims, shards, -0.22, 0.18)
    return jnp.clip(spiked(values, jax.random.fold_in(stream_key, 3), *heavy), -bound, bound).astype(kind)


def setup_inputs(seed: int = 0, part: int = 0) -> dict:
    keys = jax.random.split(jax.random.key(seed), 5)
    own_keys = jax.random.split(jax.random.fold_in(keys[4], part), 5)
    return {
        "volume": noise(own_keys[0], (CHANNELS, DEPTH, HEIGHT, WIDTH), 1.0, 6.0, ((1, 16),)),
        "weight_two": noise(keys[1], (CHANNELS, CHANNELS, 3, 3, 3), (27 * CHANNELS) ** -0.5, 0.21875),
        "weight_three": noise(keys[2], (FILTERS, CHANNELS, 3, 3, 3), (27 * CHANNELS) ** -0.5, 0.21875),
        "cotangent": gaussian_with(own_keys[3], (FILTERS, DEPTH_HALF, HEIGHT_HALF, WIDTH_HALF), 1.0, 6.0, ((1, 16),), (1, 0, 16, 2.0)),
    }


layout_names = ('NCDHW', 'OIDHW', 'NCDHW')

def convolve(field, kernel):
    return lax.conv_general_dilated(field.astype(jnp.float32)[None], kernel.astype(jnp.float32), (1, 1, 1), [(1, 1), (1, 1), (1, 1)], dimension_numbers=layout_names, precision=lax.Precision.HIGHEST)[0]

def mirrored(kernel):
    return jnp.flip(jnp.transpose(kernel, (1, 0, 2, 3, 4)), (2, 3, 4))

def kernel_grad(field, upstream):
    padded = jnp.pad(field.astype(jnp.float32), ((0, 0), (1, 1), (1, 1), (1, 1)))
    result = lax.conv_general_dilated(padded[:, None], upstream.astype(jnp.float32)[:, None], (1, 1, 1), 'VALID', dimension_numbers=layout_names, precision=lax.Precision.HIGHEST)
    return jnp.transpose(result, (1, 0, 2, 3, 4))

def silu_slope(values):
    sigma = jax.nn.sigmoid(values)
    return sigma * (1.0 + values * (1.0 - sigma))

def reference(volume, weight_two, weight_three, cotangent):
    before = convolve(volume, weight_two)
    active = jax.nn.silu(before).astype(jnp.bfloat16)
    shape = active.shape
    pooled = active.astype(jnp.float32).reshape(shape[0], shape[1] // 2, 2, shape[2] // 2, 2, shape[3] // 2, 2).mean(axis=(2, 4, 6)).astype(jnp.bfloat16)
    features_three = convolve(pooled, weight_three).astype(jnp.bfloat16)
    grad_three = kernel_grad(pooled, cotangent)
    back_pooled = convolve(cotangent, mirrored(weight_three)).astype(jnp.bfloat16)
    spread = jnp.repeat(jnp.repeat(jnp.repeat(back_pooled.astype(jnp.float32), 2, 1), 2, 2), 2, 3) * 0.125
    back_before = (spread * silu_slope(before)).astype(jnp.bfloat16)
    grad_two = kernel_grad(volume, back_before)
    grad_volume = convolve(back_before, mirrored(weight_two)).astype(jnp.bfloat16)
    return (features_three, grad_three, grad_two, grad_volume)
```

```python
import functools

import jax
import jax.numpy as jnp
from jax import lax
from jax.experimental import pallas as pl
from jax.experimental.pallas import tpu as pltpu
from jax.sharding import PartitionSpec as P

F32 = jnp.float32
BF16 = jnp.bfloat16
MESH = pl.DeviceIdType.MESH
NN = (((1,), (0,)), ((), ()))
NT = (((1,), (1,)), ((), ()))


def dot(a, b, dims=NN):
    return lax.dot_general(a, b, dims, preferred_element_type=F32)


def eye(n):
    return (
        lax.broadcasted_iota(jnp.int32, (n, n), 0) == lax.broadcasted_iota(jnp.int32, (n, n), 1)
    ).astype(BF16)


def lane_concat(ref):
    return jnp.concatenate([ref[t].astype(F32) for t in range(ref.shape[0])], axis=1).astype(BF16)


def shifts(x):
    width = x.shape[1]
    lane = lax.broadcasted_iota(jnp.int32, x.shape, 1)
    before = jnp.where(lane == 0, 0.0, pltpu.roll(x, 1, 1))
    after = jnp.where(lane == width - 1, 0.0, pltpu.roll(x, width - 1, 1))
    return before.astype(BF16), x.astype(BF16), after.astype(BF16)


def rows_first(ref, value):
    for i in range(ref.shape[0]):
        ref[i] = value[:, 128 * i : 128 * (i + 1)]


def joined(ref):
    return jnp.concatenate([ref[i] for i in range(ref.shape[0])], axis=1)


def strided(ref, start, count, step):
    parts = [ref[i, pl.ds(start, count, stride=step), :] for i in range(ref.shape[0])]
    return jnp.concatenate(parts, axis=1)


def put_strided(ref, start, step, value):
    for i in range(ref.shape[0]):
        ref[i, pl.ds(start, value.shape[0], stride=step), :] = value[:, 128 * i : 128 * (i + 1)]


def put_stack(stack, z, h, x, flip):
    c = x.shape[0]
    pieces = shifts(x)
    if flip:
        pieces = pieces[::-1]
    for i, piece in enumerate(pieces):
        stack[z, h + 1, i * c : (i + 1) * c, :] = piece


def zero_rims(stack):
    planes, rows, k, w = stack.shape
    for z in range(planes):
        stack[z, 0] = jnp.zeros((k, w), BF16)
        stack[z, rows - 1] = jnp.zeros((k, w), BF16)


def window(stack, base, h, flip):
    parts = []
    k, w = stack.shape[2:]
    for dz in (2, 1, 0) if flip else (0, 1, 2):
        slab = stack[base + dz, pl.ds(h, 3)]
        if flip:
            parts += [slab[2], slab[1], slab[0]]
        else:
            parts.append(slab.reshape(3 * k, w))
    return jnp.concatenate(parts, axis=0)


def kernel(
    n,
    vol, w2, w3, cot,
    feat, g3, g2, gvol,
    rv, rc, rp, rb, pown, bown,
    xs, xb, xp, xc, tv, tc, tf, slope,
    a2, b2, a3, b3, acc2, acc3,
    g2send, g2recv, g2ag, g3send, g3recv,
    halo_send, halo_recv, s2, r2, sa, ra, s3, r3,
):
    me = lax.axis_index("gx")
    chan, planes, height, width = vol.shape
    filt, _, height_half, width_half = cot.shape
    barrier = pltpu.get_barrier_semaphore()

    def peer(j):
        return lax.rem(me + j, n)

    def greet(j, carry):
        pl.semaphore_signal(barrier, inc=1, device_id={"gx": peer(j)}, device_id_type=MESH)
        return carry

    lax.fori_loop(1, n, greet, 0)
    pl.semaphore_wait(barrier, n - 1)

    def halo(slot, up, src, dst):
        index = 2 * slot + (0 if up else 1)
        return pltpu.make_async_remote_copy(
            src_ref=src,
            dst_ref=dst.at[0 if up else 1],
            send_sem=halo_send.at[index],
            recv_sem=halo_recv.at[index],
            device_id={"gx": lax.rem(me + (1 if up else n - 1), n)},
            device_id_type=MESH,
        )

    def halo_start(slot, first, last, dst):
        @pl.when(me < n - 1)
        def _():
            halo(slot, True, last, dst).start()

        @pl.when(me > 0)
        def _():
            halo(slot, False, first, dst).start()

    def halo_arrive(slot, first, last, dst):
        @pl.when(me > 0)
        def _():
            halo(slot, True, last, dst).wait_recv()

        @pl.when(me < n - 1)
        def _():
            halo(slot, False, first, dst).wait_recv()

    def halo_sent(slot, first, last, dst):
        @pl.when(me < n - 1)
        def _():
            halo(slot, True, last, dst).wait_send()

        @pl.when(me > 0)
        def _():
            halo(slot, False, first, dst).wait_send()

    halos = (
        (0, vol.at[:, 0], vol.at[:, planes - 1], rv),
        (1, cot.at[:, 0], cot.at[:, 0], rc),
        (2, pown, pown, rp),
        (3, bown.at[0], bown.at[planes - 1], rb),
    )
    halo_start(*halos[1])
    halo_start(*halos[0])

    @pl.when(me == 0)
    def _():
        for ref in (rv, rc, rp, rb):
            ref[0] = jnp.zeros(ref.shape[1:], BF16)

    @pl.when(me == n - 1)
    def _():
        for ref in (rv, rc, rp, rb):
            ref[1] = jnp.zeros(ref.shape[1:], BF16)

    for stack in (xs, xb, xp, xc):
        zero_rims(stack)
    a2[...] = lane_concat(w2)
    b3[...] = lane_concat(w3)
    b2[...] = dot(eye(chan), w2[...].reshape(-1, chan), NT).astype(BF16)
    a3[...] = dot(eye(filt), w3[...].reshape(-1, filt), NT).astype(BF16)

    def build_fine(value, z):
        rows_first(tv, value.astype(F32).reshape(chan * height, width))

        def row(h, carry):
            put_stack(xs, z, h, strided(tv, h, chan, height), False)
            return carry

        lax.fori_loop(0, height, row, 0)

    def build_cot(value, z):
        rows_first(tc, value.astype(F32).reshape(filt * height_half, width_half))

        def row(h, carry):
            put_stack(xc, z, h, strided(tc, h, filt, height_half), True)
            return carry

        lax.fori_loop(0, height_half, row, 0)

    build_cot(cot[:, 0], 1)
    for d in range(planes):
        build_fine(vol[:, d], d + 1)
    halo_arrive(*halos[1])
    build_cot(rc[0], 0)
    build_cot(rc[1], 2)
    halo_arrive(*halos[0])
    build_fine(rv[0], 0)
    build_fine(rv[1], planes + 1)

    fine = lax.broadcasted_iota(jnp.int32, (width, width_half), 0)
    coarse = lax.broadcasted_iota(jnp.int32, (width, width_half), 1)
    pool = ((fine == 2 * coarse) | (fine == 2 * coarse + 1)).astype(BF16)

    def forward(hc, carry):
        total = jnp.zeros((chan, width), F32)
        for d in range(planes):
            for e in range(2):
                h = 2 * hc + e
                before = dot(a2[...], window(xs, d, h, False))
                sigma = jax.nn.sigmoid(before)
                slope[d, h] = sigma * (1.0 + before * (1.0 - sigma)) * 0.125
                total = total + (before * sigma).astype(BF16).astype(F32)
        high = total.astype(BF16)
        low = (total - high.astype(F32)).astype(BF16)
        pooled = ((dot(high, pool) + dot(low, pool)) * 0.125).astype(BF16)
        pown[hc] = pooled
        put_stack(xp, 1, hc, pooled.astype(F32), False)
        return carry

    lax.fori_loop(0, height_half, forward, 0)
    halo_start(*halos[2])

    def backward(hc, carry):
        back = dot(b3[...], window(xc, 0, hc, True)).astype(BF16)
        spread = dot(back, pool, NT)
        for d in range(planes):
            for e in range(2):
                h = 2 * hc + e
                value = (spread * slope[d, h]).astype(BF16)
                bown[d, h] = value
                put_stack(xb, d + 1, h, value.astype(F32), True)
        return carry

    lax.fori_loop(0, height_half, backward, 0)
    halo_start(*halos[3])

    k2 = a2.shape[1]
    acc2[...] = jnp.zeros(acc2.shape, F32)

    def weight_two(h, carry):
        for d in range(planes):
            acc2[:, :k2] += dot(bown[d, h], window(xs, d, h, False), NT)
        return carry

    lax.fori_loop(0, height, weight_two, 0)

    rows = acc2.shape[0] // 8
    units = rows * (acc2.shape[1] // 128)
    per = g2send.shape[1] // 8

    def place(u):
        j, r = u // rows, u % rows
        return (slice(8 * r, 8 * r + 8), slice(128 * j, 128 * j + 128))

    for u in range(n * per):
        at = (u // per, slice(u % per * 8, u % per * 8 + 8))
        g2send[at] = acc2[place(u)] if u < units else jnp.zeros((8, 128), F32)

    def scatter(send, recv, ssem, rsem, k, s):
        return pltpu.make_async_remote_copy(
            src_ref=send.at[k],
            dst_ref=recv.at[s],
            send_sem=ssem.at[k],
            recv_sem=rsem.at[s],
            device_id={"gx": k},
            device_id_type=MESH,
        )

    def start_all(send, recv, ssem, rsem):
        def one(j, carry):
            scatter(send, recv, ssem, rsem, peer(j), me).start()
            return carry

        lax.fori_loop(1, n, one, 0)

    def wait_sends(send, recv, ssem, rsem):
        def one(j, carry):
            scatter(send, recv, ssem, rsem, peer(j), me).wait_send()
            return carry

        lax.fori_loop(1, n, one, 0)

    def sum_all(send, recv, ssem, rsem):
        def one(j, total):
            s = peer(j)
            scatter(send, recv, ssem, rsem, s, s).wait_recv()
            return total + recv[s]

        return lax.fori_loop(1, n, one, send[me])

    halo_arrive(*halos[2])
    for z in range(2):

        def pooled_row(h, carry, z=z):
            put_stack(xp, 2 * z, h, rp[z, h].astype(F32), False)
            return carry

        lax.fori_loop(0, height_half, pooled_row, 0)
    start_all(g2send, g2recv, s2, r2)

    acc3[...] = jnp.zeros(acc3.shape, F32)

    def weight_three(h, carry):
        acc3[...] += dot(xc[1, h + 1, filt : 2 * filt, :], window(xp, 0, h, False), NT)
        return carry

    lax.fori_loop(0, height_half, weight_three, 0)
    own = filt // n
    for i in range(n):
        g3send[i] = acc3[i * own : (i + 1) * own, :]

    def features(h, carry):
        put_strided(tf, h, height_half, dot(a3[...], window(xp, 0, h, False)))
        return carry

    lax.fori_loop(0, height_half, features, 0)
    feat[:, 0] = joined(tf).reshape(filt, height_half, width_half).astype(BF16)
    start_all(g3send, g3recv, s3, r3)

    g2ag[me] = sum_all(g2send, g2recv, s2, r2)

    halo_arrive(*halos[3])
    for z in range(2):

        def back_row(h, carry, z=z):
            put_stack(xb, (planes + 1) * z, h, rb[z, h].astype(F32), True)
            return carry

        lax.fori_loop(0, height, back_row, 0)

    def gather(k, s):
        return pltpu.make_async_remote_copy(
            src_ref=g2ag.at[s],
            dst_ref=g2ag.at[s],
            send_sem=sa.at[k],
            recv_sem=ra.at[s],
            device_id={"gx": k},
            device_id_type=MESH,
        )

    def gather_start(j, carry):
        gather(peer(j), me).start()
        return carry

    lax.fori_loop(1, n, gather_start, 0)

    for d in range(planes):

        def volume_row(h, carry, d=d):
            put_strided(tv, h, height, dot(b2[...], window(xb, d, h, True)))
            return carry

        lax.fori_loop(0, height, volume_row, 0)
        gvol[:, d] = joined(tv).reshape(chan, height, width).astype(BF16)

    taps = w2.shape[0]
    total = sum_all(g3send, g3recv, s3, r3)
    for t in range(taps):
        g3[t] = total[:, chan * t : chan * (t + 1)]

    def gather_wait(j, carry):
        gather(peer(j), peer(j)).wait_recv()
        return carry

    lax.fori_loop(1, n, gather_wait, 0)
    for u in range(units):
        acc2[place(u)] = g2ag[u // per, u % per * 8 : u % per * 8 + 8]
    for t in range(taps):
        g2[t] = acc2[:, chan * t : chan * (t + 1)]

    for item in halos:
        halo_sent(*item)
    wait_sends(g2send, g2recv, s2, r2)
    wait_sends(g3send, g3recv, s3, r3)

    def gather_sent(j, carry):
        gather(peer(j), me).wait_send()
        return carry

    lax.fori_loop(1, n, gather_sent, 0)


def local(n, volume, weight_two, weight_three, cotangent):
    chan, planes, height, width = volume.shape
    filt, _, height_half, width_half = cotangent.shape
    taps = 27
    w2 = jnp.transpose(weight_two, (2, 3, 4, 0, 1)).reshape(taps, chan, chan)
    w3 = jnp.transpose(weight_three, (2, 3, 4, 1, 0)).reshape(taps, chan, filt)
    k2 = taps * chan
    k2pad = -(-k2 // 128) * 128
    units = chan // 8 * (k2pad // 128)
    per = -(-units // n)
    own = filt // n
    dma = pltpu.SemaphoreType.DMA
    vmem = pl.BlockSpec(memory_space=pltpu.VMEM)
    feat, g3, g2, gvol = pl.pallas_call(
        functools.partial(kernel, n),
        out_shape=(
            jax.ShapeDtypeStruct(cotangent.shape, BF16),
            jax.ShapeDtypeStruct((taps, own, chan), F32),
            jax.ShapeDtypeStruct((taps, chan, chan), F32),
            jax.ShapeDtypeStruct(volume.shape, BF16),
        ),
        in_specs=[vmem] * 4,
        out_specs=(vmem,) * 4,
        scratch_shapes=[
            pltpu.VMEM((2, chan, height, width), BF16),
            pltpu.VMEM((2, filt, height_half, width_half), BF16),
            pltpu.VMEM((2, height_half, chan, width_half), BF16),
            pltpu.VMEM((2, height, chan, width), BF16),
            pltpu.VMEM((height_half, chan, width_half), BF16),
            pltpu.VMEM((planes, height, chan, width), BF16),
            pltpu.VMEM((planes + 2, height + 2, 3 * chan, width), BF16),
            pltpu.VMEM((planes + 2, height + 2, 3 * chan, width), BF16),
            pltpu.VMEM((3, height_half + 2, 3 * chan, width_half), BF16),
            pltpu.VMEM((3, height_half + 2, 3 * filt, width_half), BF16),
            pltpu.VMEM((width // 128, chan * height, 128), F32),
            pltpu.VMEM((width_half // 128, filt * height_half, 128), F32),
            pltpu.VMEM((width_half // 128, filt * height_half, 128), F32),
            pltpu.VMEM((planes, height, chan, width), F32),
            pltpu.VMEM((chan, k2), BF16),
            pltpu.VMEM((chan, k2), BF16),
            pltpu.VMEM((filt, k2), BF16),
            pltpu.VMEM((chan, taps * filt), BF16),
            pltpu.VMEM((chan, k2pad), F32),
            pltpu.VMEM((filt, k2), F32),
            pltpu.VMEM((n, per * 8, 128), F32),
            pltpu.VMEM((n, per * 8, 128), F32),
            pltpu.VMEM((n, per * 8, 128), F32),
            pltpu.VMEM((n, own, k2), F32),
            pltpu.VMEM((n, own, k2), F32),
            dma((8,)), dma((8,)),
            dma((n,)), dma((n,)), dma((n,)), dma((n,)), dma((n,)), dma((n,)),
        ],
        compiler_params=pltpu.CompilerParams(
            collective_id=0, has_side_effects=True, vmem_limit_bytes=48 << 20
        ),
    )(volume, w2, w3, cotangent)

    def taps_last(grad):
        return jnp.transpose(grad.reshape(3, 3, 3, *grad.shape[1:]), (3, 4, 0, 1, 2))

    return feat, taps_last(g3), taps_last(g2), gvol


def solution(mesh):
    return jax.shard_map(
        functools.partial(local, mesh.shape["gx"]),
        mesh=mesh,
        in_specs=(
            P(None, ("groups", "gx"), None, None),
            P(),
            P(),
            P(None, ("groups", "gx"), None, None),
        ),
        out_specs=(
            P(None, ("groups", "gx"), None, None),
            P(("groups", "gx"), None, None, None, None),
            P("groups", None, None, None, None),
            P(None, ("groups", "gx"), None, None),
        ),
        check_vma=False,
    )
```

```python
import functools

import jax
import jax.numpy as jnp
from jax import lax
from jax.experimental import pallas as pl
from jax.experimental.pallas import tpu as pltpu
from jax.sharding import PartitionSpec as P

F32 = jnp.float32
BF16 = jnp.bfloat16
MESH = pl.DeviceIdType.MESH
NN = (((1,), (0,)), ((), ()))
NT = (((1,), (1,)), ((), ()))


def dot(a, b, dims=NN):
    return lax.dot_general(a, b, dims, preferred_element_type=F32)


def eye(n):
    return (
        lax.broadcasted_iota(jnp.int32, (n, n), 0) == lax.broadcasted_iota(jnp.int32, (n, n), 1)
    ).astype(BF16)


def lane_concat(parts):
    return jnp.concatenate([part.astype(F32) for part in parts], axis=1).astype(BF16)


def lanes(x, period):
    return lax.rem(lax.broadcasted_iota(jnp.int32, x.shape, 1), period)


def before_of(x, period):
    return jnp.where(lanes(x, period) == 0, 0.0, pltpu.roll(x, 1, 1))


def after_of(x, period):
    return jnp.where(lanes(x, period) == period - 1, 0.0, pltpu.roll(x, x.shape[1] - 1, 1))


def gathered(y, at, count, period, flip):
    first, mid, last = (y[at + i * count : at + (i + 1) * count] for i in range(3))
    if flip:
        first, last = last, first
    return before_of(first, period) + mid + after_of(last, period)


def rows_first(ref, value):
    for i in range(ref.shape[0]):
        ref[i] = value[:, 128 * i : 128 * (i + 1)]


def joined(ref):
    return jnp.concatenate([ref[i] for i in range(ref.shape[0])], axis=1)


def strided(ref, start, count, step):
    parts = [ref[i, pl.ds(start, count, stride=step), :] for i in range(ref.shape[0])]
    return jnp.concatenate(parts, axis=1)


def put_strided(ref, start, step, value):
    for i in range(ref.shape[0]):
        ref[i, pl.ds(start, value.shape[0], stride=step), :] = value[:, 128 * i : 128 * (i + 1)]


def zero_rims(stack):
    planes, rows, k, w = stack.shape
    for z in range(planes):
        stack[z, 0] = jnp.zeros((k, w), BF16)
        stack[z, rows - 1] = jnp.zeros((k, w), BF16)


def pair(stack, h):
    k, w = stack.shape[2:]
    rows = stack.shape[0] * 3 * k
    left = stack[:, pl.ds(h, 3)].reshape(rows, w)
    right = stack[:, pl.ds(h + 1, 3)].reshape(rows, w)
    return jnp.concatenate([left, right], axis=1)


def kernel(
    n,
    vol_in, w2_in, w3_in, cot_in,
    feat, g3, g2, gvol,
    vol, w2, w3, cot,
    xs, xb, xp, xc, bs, cs, tv, tc, slope,
    a2, b2, a3, b3, acc2, acc3, tail,
    g2send, g2recv, g2ag, g3send, g3recv,
    load, halo_send, halo_recv, s2, r2, sa, ra, s3, r3,
):
    me = lax.axis_index("gx")
    chan, planes, height, width = vol.shape
    filt, _, height_half, width_half = cot.shape
    barrier = pltpu.get_barrier_semaphore()
    loads = [
        pltpu.make_async_copy(src, dst, load.at[i])
        for i, (src, dst) in enumerate(((cot_in, cot), (vol_in, vol), (w2_in, w2), (w3_in, w3)))
    ]
    for copy in loads:
        copy.start()

    def peer(j):
        return lax.rem(me + j, n)

    def greet(j, carry):
        pl.semaphore_signal(barrier, inc=1, device_id={"gx": peer(j)}, device_id_type=MESH)
        return carry

    lax.fori_loop(1, n, greet, 0)

    def halo(slot, up, stack):
        index = 2 * slot + (0 if up else 1)
        last = stack.shape[0] - 1
        rows = pl.ds(1, stack.shape[1] - 2)
        return pltpu.make_async_remote_copy(
            src_ref=stack.at[last - 1 if up else 1, rows],
            dst_ref=stack.at[0 if up else last, rows],
            send_sem=halo_send.at[index],
            recv_sem=halo_recv.at[index],
            device_id={"gx": lax.rem(me + (1 if up else n - 1), n)},
            device_id_type=MESH,
        )

    def halo_start(slot, stack):
        @pl.when(me < n - 1)
        def _():
            halo(slot, True, stack).start()

        @pl.when(me > 0)
        def _():
            halo(slot, False, stack).start()

    def halo_arrive(slot, stack):
        @pl.when(me > 0)
        def _():
            halo(slot, True, stack).wait_recv()

        @pl.when(me < n - 1)
        def _():
            halo(slot, False, stack).wait_recv()

    def halo_sent(slot, stack):
        @pl.when(me < n - 1)
        def _():
            halo(slot, True, stack).wait_send()

        @pl.when(me > 0)
        def _():
            halo(slot, False, stack).wait_send()

    halos = ((0, xs), (1, xc), (2, xp), (3, xb))

    loads[0].wait()
    rows_first(tc, cot[:, 0].astype(F32).reshape(filt * height_half, width_half))

    def cot_row(h, carry):
        x = strided(tc, h, filt, height_half)
        xc[1, h + 1] = x.astype(BF16)
        cs[h, 0:filt] = after_of(x, width_half).astype(BF16)
        cs[h, filt : 2 * filt] = x.astype(BF16)
        cs[h, 2 * filt : 3 * filt] = before_of(x, width_half).astype(BF16)
        return carry

    lax.fori_loop(0, height_half, cot_row, 0)
    loads[1].wait()
    for d in range(planes):
        rows_first(tv.at[d], vol[:, d].astype(F32).reshape(chan * height, width))

        def vol_row(h, carry, d=d):
            xs[d + 1, h + 1] = strided(tv.at[d], h, chan, height).astype(BF16)
            return carry

        lax.fori_loop(0, height, vol_row, 0)
    for stack in (xs, xb, xp, xc):
        zero_rims(stack)
    pl.semaphore_wait(barrier, n - 1)
    halo_start(*halos[0])
    halo_start(*halos[1])

    @pl.when(me == 0)
    def _():
        for _, stack in halos:
            stack[0] = jnp.zeros(stack.shape[1:], BF16)

    @pl.when(me == n - 1)
    def _():
        for _, stack in halos:
            stack[stack.shape[0] - 1] = jnp.zeros(stack.shape[1:], BF16)

    loads[2].wait()
    loads[3].wait()
    hole = jnp.zeros((chan, chan), BF16)
    gap = jnp.zeros((chan, 4 * chan), BF16)
    for e in range(2):
        for i in range(3):
            ahead, back = [], []
            for dz in range(3):
                for y in range(4):
                    inside = 0 <= y - e <= 2
                    ahead.append(w2[9 * dz + 3 * (y - e) + i] if inside else hole)
                    back.append(w2[9 * (2 - dz) + 3 * (2 - y + e) + i] if inside else hole)
            group = lane_concat(ahead)
            flipped = dot(eye(chan), jnp.concatenate(back, axis=0), NT).astype(BF16)
            for d in range(planes):
                rows = slice(((2 * d + e) * 3 + i) * chan, ((2 * d + e) * 3 + i + 1) * chan)
                for big, part in ((a2, group), (b2, flipped)):
                    line = [gap] * d + [part] + [gap] * (planes - 1 - d)
                    big[rows, :] = jnp.concatenate(line, axis=1)
    for i in range(3):
        taps_in = [w3[3 * t + i] for t in range(9)]
        taps_out = [w3[3 * (8 - t) + i] for t in range(9)]
        b3[i * chan : (i + 1) * chan, :] = lane_concat(taps_out)
        a3[i * filt : (i + 1) * filt, :] = dot(
            eye(filt), jnp.concatenate(taps_in, axis=0), NT
        ).astype(BF16)

    fine = lax.broadcasted_iota(jnp.int32, (width, width_half), 0)
    coarse = lax.broadcasted_iota(jnp.int32, (width, width_half), 1)
    pool = ((fine == 2 * coarse) | (fine == 2 * coarse + 1)).astype(BF16)

    halo_arrive(*halos[0])

    def forward(hc, carry):
        x = xs[:, pl.ds(2 * hc, 4)].reshape((planes + 2) * 4 * chan, width)
        y = dot(a2[...], x)
        total = jnp.zeros((chan, width), F32)
        for d in range(planes):
            for e in range(2):
                before = gathered(y, (2 * d + e) * 3 * chan, chan, width, False)
                sigma = jax.nn.sigmoid(before)
                slope[d, 2 * hc + e] = sigma * (1.0 + before * (1.0 - sigma)) * 0.125
                total = total + (before * sigma).astype(BF16).astype(F32)
        high = total.astype(BF16)
        low = (total - high.astype(F32)).astype(BF16)
        xp[1, hc + 1] = ((dot(high, pool) + dot(low, pool)) * 0.125).astype(BF16)
        return carry

    lax.fori_loop(0, height_half, forward, 0)
    halo_arrive(*halos[1])
    halo_start(*halos[2])

    def backward(hq, carry):
        y = dot(b3[...], pair(xc, 2 * hq))
        back = gathered(y, 0, chan, width_half, True).astype(BF16)
        for q in range(2):
            spread = dot(back[:, q * width_half : (q + 1) * width_half], pool, NT)
            for d in range(planes):
                for e in range(2):
                    h = 4 * hq + 2 * q + e
                    value = (spread * slope[d, h]).astype(BF16)
                    wide = value.astype(F32)
                    xb[d + 1, h + 1] = value
                    bs[d, h, 0:chan] = after_of(wide, width).astype(BF16)
                    bs[d, h, chan : 2 * chan] = value
                    bs[d, h, 2 * chan : 3 * chan] = before_of(wide, width).astype(BF16)
        return carry

    lax.fori_loop(0, height_half // 2, backward, 0)

    def weight_two(h, total):
        for d in range(planes):
            x = xs[d : d + 3, pl.ds(h, 3)].reshape(9 * chan, width)
            total = total + dot(bs[d, h], x, NT)
        return total

    acc2[...] = weight_two(0, jnp.zeros(acc2.shape, F32))
    halo_start(*halos[3])

    def more_two(h, carry):
        acc2[...] = weight_two(h, acc2[...])
        return carry

    lax.fori_loop(1, height, more_two, 0)

    full = acc2.shape[1] // 128
    rest = acc2.shape[1] - 128 * full
    groups = acc2.shape[0] // 8
    units = full * groups + chan // 8
    per = g2send.shape[1] // 8
    tail[...] = jnp.concatenate(
        [acc2[i * chan : (i + 1) * chan, 128 * full :] for i in range(3)]
        + [jnp.zeros((chan, 128 - 3 * rest), F32)],
        axis=1,
    )

    def place(u):
        j, r = u // groups, u % groups
        if j == full:
            return tail, (slice(8 * r, 8 * r + 8), slice(0, 128))
        return acc2, (slice(8 * r, 8 * r + 8), slice(128 * j, 128 * j + 128))

    for u in range(n * per):
        at = (u // per, slice(u % per * 8, u % per * 8 + 8))
        if u < units:
            ref, where = place(u)
            g2send[at] = ref[where]
        else:
            g2send[at] = jnp.zeros((8, 128), F32)

    def scatter(send, recv, ssem, rsem, k, s):
        return pltpu.make_async_remote_copy(
            src_ref=send.at[k],
            dst_ref=recv.at[s],
            send_sem=ssem.at[k],
            recv_sem=rsem.at[s],
            device_id={"gx": k},
            device_id_type=MESH,
        )

    def start_all(send, recv, ssem, rsem):
        def one(j, carry):
            scatter(send, recv, ssem, rsem, peer(j), me).start()
            return carry

        lax.fori_loop(1, n, one, 0)

    def wait_sends(send, recv, ssem, rsem):
        def one(j, carry):
            scatter(send, recv, ssem, rsem, peer(j), me).wait_send()
            return carry

        lax.fori_loop(1, n, one, 0)

    def sum_all(send, recv, ssem, rsem):
        def one(j, total):
            s = peer(j)
            scatter(send, recv, ssem, rsem, s, s).wait_recv()
            return total + recv[s]

        return lax.fori_loop(1, n, one, send[me])

    halo_arrive(*halos[2])
    start_all(g2send, g2recv, s2, r2)

    acc3[...] = jnp.zeros(acc3.shape, F32)

    def weight_three(hq, carry):
        upstream = jnp.concatenate([cs[2 * hq], cs[2 * hq + 1]], axis=1)
        acc3[...] += dot(upstream, pair(xp, 2 * hq), NT)
        return carry

    lax.fori_loop(0, height_half // 2, weight_three, 0)
    own = filt // n
    for k in range(n):
        for i in range(3):
            g3send[k, i] = acc3[i * filt + k * own : i * filt + (k + 1) * own, :]

    def features(hq, carry):
        y = gathered(dot(a3[...], pair(xp, 2 * hq)), 0, filt, width_half, False)
        for q in range(2):
            put_strided(tc, 2 * hq + q, height_half, y[:, q * width_half : (q + 1) * width_half])
        return carry

    lax.fori_loop(0, height_half // 2, features, 0)
    feat[:, 0] = joined(tc).reshape(filt, height_half, width_half).astype(BF16)
    start_all(g3send, g3recv, s3, r3)

    g2ag[me] = sum_all(g2send, g2recv, s2, r2)
    halo_arrive(*halos[3])

    def gather(k, s):
        return pltpu.make_async_remote_copy(
            src_ref=g2ag.at[s],
            dst_ref=g2ag.at[s],
            send_sem=sa.at[k],
            recv_sem=ra.at[s],
            device_id={"gx": k},
            device_id_type=MESH,
        )

    def gather_start(j, carry):
        gather(peer(j), me).start()
        return carry

    lax.fori_loop(1, n, gather_start, 0)

    def volume_row(hc, carry):
        x = xb[:, pl.ds(2 * hc, 4)].reshape((planes + 2) * 4 * chan, width)
        y = dot(b2[...], x)
        for d in range(planes):
            for e in range(2):
                value = gathered(y, (2 * d + e) * 3 * chan, chan, width, True)
                put_strided(tv.at[d], 2 * hc + e, height, value)
        return carry

    lax.fori_loop(0, height_half, volume_row, 0)
    for d in range(planes):
        gvol[:, d] = joined(tv.at[d]).reshape(chan, height, width).astype(BF16)

    total = sum_all(g3send, g3recv, s3, r3)
    for t in range(27):
        g3[t] = total[t % 3, :, chan * (t // 3) : chan * (t // 3 + 1)]

    def gather_wait(j, carry):
        gather(peer(j), peer(j)).wait_recv()
        return carry

    lax.fori_loop(1, n, gather_wait, 0)
    for u in range(units):
        ref, where = place(u)
        ref[where] = g2ag[u // per, u % per * 8 : u % per * 8 + 8]
    for t in range(27):
        i, j = t % 3, t // 3
        if chan * j < 128 * full:
            g2[t] = acc2[i * chan : (i + 1) * chan, chan * j : chan * (j + 1)]
        else:
            g2[t] = tail[:, i * rest : (i + 1) * rest]

    for item in halos:
        halo_sent(*item)
    wait_sends(g2send, g2recv, s2, r2)
    wait_sends(g3send, g3recv, s3, r3)

    def gather_sent(j, carry):
        gather(peer(j), me).wait_send()
        return carry

    lax.fori_loop(1, n, gather_sent, 0)


def local(n, volume, weight_two, weight_three, cotangent):
    chan, planes, height, width = volume.shape
    filt, _, height_half, width_half = cotangent.shape
    taps = 27
    w2 = jnp.transpose(weight_two, (2, 3, 4, 0, 1)).reshape(taps, chan, chan)
    w3 = jnp.transpose(weight_three, (2, 3, 4, 1, 0)).reshape(taps, chan, filt)
    units = 3 * chan // 8 * (9 * chan // 128) + chan // 8
    per = -(-units // n)
    own = filt // n
    wide = (planes + 2) * 4 * chan
    tall = planes * 2 * 3 * chan
    dma = pltpu.SemaphoreType.DMA
    vmem = pl.BlockSpec(memory_space=pltpu.VMEM)
    hbm = pl.BlockSpec(memory_space=pltpu.HBM)
    feat, g3, g2, gvol = pl.pallas_call(
        functools.partial(kernel, n),
        out_shape=(
            jax.ShapeDtypeStruct(cotangent.shape, BF16),
            jax.ShapeDtypeStruct((taps, own, chan), F32),
            jax.ShapeDtypeStruct((taps, chan, chan), F32),
            jax.ShapeDtypeStruct(volume.shape, BF16),
        ),
        in_specs=[hbm] * 4,
        out_specs=(vmem,) * 4,
        scratch_shapes=[
            pltpu.VMEM(volume.shape, BF16),
            pltpu.VMEM(w2.shape, BF16),
            pltpu.VMEM(w3.shape, BF16),
            pltpu.VMEM(cotangent.shape, BF16),
            pltpu.VMEM((planes + 2, height + 2, chan, width), BF16),
            pltpu.VMEM((planes + 2, height + 2, chan, width), BF16),
            pltpu.VMEM((3, height_half + 2, chan, width_half), BF16),
            pltpu.VMEM((3, height_half + 2, filt, width_half), BF16),
            pltpu.VMEM((planes, height, 3 * chan, width), BF16),
            pltpu.VMEM((height_half, 3 * filt, width_half), BF16),
            pltpu.VMEM((planes, width // 128, chan * height, 128), F32),
            pltpu.VMEM((width_half // 128, filt * height_half, 128), F32),
            pltpu.VMEM((planes, height, chan, width), F32),
            pltpu.VMEM((tall, wide), BF16),
            pltpu.VMEM((tall, wide), BF16),
            pltpu.VMEM((3 * filt, 9 * chan), BF16),
            pltpu.VMEM((3 * chan, 9 * filt), BF16),
            pltpu.VMEM((3 * chan, 9 * chan), F32),
            pltpu.VMEM((3 * filt, 9 * chan), F32),
            pltpu.VMEM((chan, 128), F32),
            pltpu.VMEM((n, per * 8, 128), F32),
            pltpu.VMEM((n, per * 8, 128), F32),
            pltpu.VMEM((n, per * 8, 128), F32),
            pltpu.VMEM((n, 3, own, 9 * chan), F32),
            pltpu.VMEM((n, 3, own, 9 * chan), F32),
            dma((4,)), dma((8,)), dma((8,)),
            dma((n,)), dma((n,)), dma((n,)), dma((n,)), dma((n,)), dma((n,)),
        ],
        compiler_params=pltpu.CompilerParams(
            collective_id=0, has_side_effects=True, vmem_limit_bytes=48 << 20
        ),
    )(volume, w2, w3, cotangent)

    def taps_last(grad):
        return jnp.transpose(grad.reshape(3, 3, 3, *grad.shape[1:]), (3, 4, 0, 1, 2))

    return feat, taps_last(g3), taps_last(g2), gvol


def solution(mesh):
    return jax.shard_map(
        functools.partial(local, mesh.shape["gx"]),
        mesh=mesh,
        in_specs=(
            P(None, ("groups", "gx"), None, None),
            P(),
            P(),
            P(None, ("groups", "gx"), None, None),
        ),
        out_specs=(
            P(None, ("groups", "gx"), None, None),
            P(("groups", "gx"), None, None, None, None),
            P("groups", None, None, None, None),
            P(None, ("groups", "gx"), None, None),
        ),
        check_vma=False,
    )
```

```python
import functools

import jax
import jax.numpy as jnp
from jax import lax
from jax.experimental import pallas as pl
from jax.experimental.pallas import tpu as pltpu
from jax.sharding import PartitionSpec as P

F32 = jnp.float32
BF16 = jnp.bfloat16
MESH = pl.DeviceIdType.MESH
NN = (((1,), (0,)), ((), ()))
NT = (((1,), (1,)), ((), ()))


def dot(a, b, dims=NN):
    return lax.dot_general(a, b, dims, preferred_element_type=F32)


def eye(n):
    return (
        lax.broadcasted_iota(jnp.int32, (n, n), 0) == lax.broadcasted_iota(jnp.int32, (n, n), 1)
    ).astype(BF16)


def lane_concat(parts):
    return jnp.concatenate([part.astype(F32) for part in parts], axis=1).astype(BF16)


def lanes(x, period):
    return lax.rem(lax.broadcasted_iota(jnp.int32, x.shape, 1), period)


def before_of(x, period):
    return jnp.where(lanes(x, period) == 0, 0.0, pltpu.roll(x, 1, 1))


def after_of(x, period):
    return jnp.where(lanes(x, period) == period - 1, 0.0, pltpu.roll(x, x.shape[1] - 1, 1))


def gathered(y, at, count, period, flip):
    first, mid, last = (y[at + i * count : at + (i + 1) * count] for i in range(3))
    if flip:
        first, last = last, first
    return before_of(first, period) + mid + after_of(last, period)


def rows_first(ref, value):
    for i in range(ref.shape[0]):
        ref[i] = value[:, 128 * i : 128 * (i + 1)]


def joined(ref):
    return jnp.concatenate([ref[i] for i in range(ref.shape[0])], axis=1)


def strided(ref, start, count, step):
    parts = [ref[i, pl.ds(start, count, stride=step), :] for i in range(ref.shape[0])]
    return jnp.concatenate(parts, axis=1)


def put_strided(ref, start, step, value):
    for i in range(ref.shape[0]):
        ref[i, pl.ds(start, value.shape[0], stride=step), :] = value[:, 128 * i : 128 * (i + 1)]


def zero_rims(stack):
    planes, rows, k, w = stack.shape
    for z in range(planes):
        stack[z, 0] = jnp.zeros((k, w), BF16)
        stack[z, rows - 1] = jnp.zeros((k, w), BF16)


def pair(stack, h):
    k, w = stack.shape[2:]
    rows = stack.shape[0] * 3 * k
    left = stack[:, pl.ds(h, 3)].reshape(rows, w)
    right = stack[:, pl.ds(h + 1, 3)].reshape(rows, w)
    return jnp.concatenate([left, right], axis=1)


def kernel(
    n,
    vol_in, w2_in, w3_in, cot_in,
    feat, g3, g2, gvol,
    vol, w2, w3, cot,
    xs, xb, xp, xc, bs, cs, tv, tc, backs,
    a2, b2, a3, b3, acc2, acc3, tail,
    g2send, g2recv, g2ag, g3send, g3recv,
    load, halo_send, halo_recv, s2, r2, sa, ra, s3, r3,
):
    me = lax.axis_index("gx")
    chan, planes, height, width = vol.shape
    filt, _, height_half, width_half = cot.shape
    barrier = pltpu.get_barrier_semaphore()
    loads = [
        pltpu.make_async_copy(src, dst, load.at[i])
        for i, (src, dst) in enumerate(((cot_in, cot), (vol_in, vol), (w2_in, w2), (w3_in, w3)))
    ]
    for copy in loads:
        copy.start()

    def peer(j):
        return lax.rem(me + j, n)

    def greet(j, carry):
        pl.semaphore_signal(barrier, inc=1, device_id={"gx": peer(j)}, device_id_type=MESH)
        return carry

    lax.fori_loop(1, n, greet, 0)

    def halo(slot, stack, part, parts, up):
        index = 2 * slot + (0 if up else 1)
        last = stack.shape[0] - 1
        count = (stack.shape[1] - 2) // parts
        rows = pl.ds(1 + part * count, count)
        return pltpu.make_async_remote_copy(
            src_ref=stack.at[last - 1 if up else 1, rows],
            dst_ref=stack.at[0 if up else last, rows],
            send_sem=halo_send.at[index],
            recv_sem=halo_recv.at[index],
            device_id={"gx": lax.rem(me + (1 if up else n - 1), n)},
            device_id_type=MESH,
        )

    def halo_start(*item):
        @pl.when(me < n - 1)
        def _():
            halo(*item, True).start()

        @pl.when(me > 0)
        def _():
            halo(*item, False).start()

    def halo_arrive(*item):
        @pl.when(me > 0)
        def _():
            halo(*item, True).wait_recv()

        @pl.when(me < n - 1)
        def _():
            halo(*item, False).wait_recv()

    def halo_sent(*item):
        @pl.when(me < n - 1)
        def _():
            halo(*item, True).wait_send()

        @pl.when(me > 0)
        def _():
            halo(*item, False).wait_send()

    halos = (
        (0, xs, 0, 2), (1, xs, 1, 2), (2, xc, 0, 1), (3, xp, 0, 1), (4, xb, 0, 2), (5, xb, 1, 2)
    )

    loads[0].wait()
    rows_first(tc, cot[:, 0].astype(F32).reshape(filt * height_half, width_half))

    def cot_row(h, carry):
        x = strided(tc, h, filt, height_half)
        xc[1, h + 1] = x.astype(BF16)
        cs[h, 0:filt] = after_of(x, width_half).astype(BF16)
        cs[h, filt : 2 * filt] = x.astype(BF16)
        cs[h, 2 * filt : 3 * filt] = before_of(x, width_half).astype(BF16)
        return carry

    lax.fori_loop(0, height_half, cot_row, 0)
    loads[1].wait()
    for d in range(planes):
        rows_first(tv.at[d], vol[:, d].astype(F32).reshape(chan * height, width))

        def vol_row(h, carry, d=d):
            xs[d + 1, h + 1] = strided(tv.at[d], h, chan, height).astype(BF16)
            return carry

        lax.fori_loop(0, height, vol_row, 0)
    for stack in (xs, xb, xp, xc):
        zero_rims(stack)
    pl.semaphore_wait(barrier, n - 1)
    halo_start(*halos[2])
    halo_start(*halos[0])
    halo_start(*halos[1])

    @pl.when(me == 0)
    def _():
        for stack in (xs, xb, xp, xc):
            stack[0] = jnp.zeros(stack.shape[1:], BF16)

    @pl.when(me == n - 1)
    def _():
        for stack in (xs, xb, xp, xc):
            stack[stack.shape[0] - 1] = jnp.zeros(stack.shape[1:], BF16)

    loads[2].wait()
    loads[3].wait()
    hole = jnp.zeros((chan, chan), BF16)
    gap = jnp.zeros((chan, 4 * chan), BF16)
    for e in range(2):
        for i in range(3):
            ahead, back = [], []
            for dz in range(3):
                for y in range(4):
                    inside = 0 <= y - e <= 2
                    ahead.append(w2[9 * dz + 3 * (y - e) + i] if inside else hole)
                    back.append(w2[9 * (2 - dz) + 3 * (2 - y + e) + i] if inside else hole)
            group = lane_concat(ahead)
            flipped = dot(eye(chan), jnp.concatenate(back, axis=0), NT).astype(BF16)
            for d in range(planes):
                rows = slice(((2 * d + e) * 3 + i) * chan, ((2 * d + e) * 3 + i + 1) * chan)
                for big, part in ((a2, group), (b2, flipped)):
                    line = [gap] * d + [part] + [gap] * (planes - 1 - d)
                    big[rows, :] = jnp.concatenate(line, axis=1)
    for i in range(3):
        taps_in = [w3[3 * t + i] for t in range(9)]
        taps_out = [w3[3 * (8 - t) + i] for t in range(9)]
        b3[i * chan : (i + 1) * chan, :] = lane_concat(taps_out)
        a3[i * filt : (i + 1) * filt, :] = dot(
            eye(filt), jnp.concatenate(taps_in, axis=0), NT
        ).astype(BF16)

    fine = lax.broadcasted_iota(jnp.int32, (width, width_half), 0)
    coarse = lax.broadcasted_iota(jnp.int32, (width, width_half), 1)
    pool = ((fine == 2 * coarse) | (fine == 2 * coarse + 1)).astype(BF16)

    halo_arrive(*halos[2])

    def coarse_back(hq, carry):
        y = dot(b3[...], pair(xc, 2 * hq))
        value = gathered(y, 0, chan, width_half, True).astype(BF16)
        for q in range(2):
            backs[2 * hq + q] = value[:, q * width_half : (q + 1) * width_half]
        return carry

    lax.fori_loop(0, height_half // 2, coarse_back, 0)

    def forward(hc, carry):
        x = xs[:, pl.ds(2 * hc, 4)].reshape((planes + 2) * 4 * chan, width)
        y = dot(a2[...], x)
        spread = dot(backs[hc], pool, NT) * 0.125
        total = jnp.zeros((chan, width), F32)
        for d in range(planes):
            for e in range(2):
                h = 2 * hc + e
                before = gathered(y, (2 * d + e) * 3 * chan, chan, width, False)
                sigma = jax.nn.sigmoid(before)
                total = total + (before * sigma).astype(BF16).astype(F32)
                value = (spread * (sigma * (1.0 + before * (1.0 - sigma)))).astype(BF16)
                wide = value.astype(F32)
                xb[d + 1, h + 1] = value
                bs[d, h, 0:chan] = after_of(wide, width).astype(BF16)
                bs[d, h, chan : 2 * chan] = value
                bs[d, h, 2 * chan : 3 * chan] = before_of(wide, width).astype(BF16)
        high = total.astype(BF16)
        low = (total - high.astype(F32)).astype(BF16)
        xp[1, hc + 1] = ((dot(high, pool) + dot(low, pool)) * 0.125).astype(BF16)
        return carry

    ready = height_half // 2 - 1
    halo_arrive(*halos[0])
    lax.fori_loop(0, ready, forward, 0)
    halo_arrive(*halos[1])
    lax.fori_loop(ready, height_half, forward, 0)

    def weight_two(h, total):
        for d in range(planes):
            x = xs[d : d + 3, pl.ds(h, 3)].reshape(9 * chan, width)
            total = total + dot(bs[d, h], x, NT)
        return total

    acc2[...] = weight_two(0, jnp.zeros(acc2.shape, F32))
    halo_start(*halos[3])
    halo_start(*halos[4])
    halo_start(*halos[5])

    def more_two(h, carry):
        acc2[...] = weight_two(h, acc2[...])
        return carry

    lax.fori_loop(1, height, more_two, 0)

    full = acc2.shape[1] // 128
    rest = acc2.shape[1] - 128 * full
    groups = acc2.shape[0] // 8
    units = full * groups + chan // 8
    per = g2send.shape[1] // 8
    tail[...] = jnp.concatenate(
        [acc2[i * chan : (i + 1) * chan, 128 * full :] for i in range(3)]
        + [jnp.zeros((chan, 128 - 3 * rest), F32)],
        axis=1,
    )

    def place(u):
        j, r = u // groups, u % groups
        if j == full:
            return tail, (slice(8 * r, 8 * r + 8), slice(0, 128))
        return acc2, (slice(8 * r, 8 * r + 8), slice(128 * j, 128 * j + 128))

    for u in range(n * per):
        at = (u // per, slice(u % per * 8, u % per * 8 + 8))
        if u < units:
            ref, where = place(u)
            g2send[at] = ref[where]
        else:
            g2send[at] = jnp.zeros((8, 128), F32)

    def scatter(send, recv, ssem, rsem, k, s):
        return pltpu.make_async_remote_copy(
            src_ref=send.at[k],
            dst_ref=recv.at[s],
            send_sem=ssem.at[k],
            recv_sem=rsem.at[s],
            device_id={"gx": k},
            device_id_type=MESH,
        )

    def start_all(send, recv, ssem, rsem):
        def one(j, carry):
            scatter(send, recv, ssem, rsem, peer(j), me).start()
            return carry

        lax.fori_loop(1, n, one, 0)

    def wait_sends(send, recv, ssem, rsem):
        def one(j, carry):
            scatter(send, recv, ssem, rsem, peer(j), me).wait_send()
            return carry

        lax.fori_loop(1, n, one, 0)

    def sum_all(send, recv, ssem, rsem):
        def one(j, total):
            s = peer(j)
            scatter(send, recv, ssem, rsem, s, s).wait_recv()
            return total + recv[s]

        return lax.fori_loop(1, n, one, send[me])

    halo_arrive(*halos[3])
    start_all(g2send, g2recv, s2, r2)

    acc3[...] = jnp.zeros(acc3.shape, F32)

    def weight_three(hq, carry):
        upstream = jnp.concatenate([cs[2 * hq], cs[2 * hq + 1]], axis=1)
        acc3[...] += dot(upstream, pair(xp, 2 * hq), NT)
        return carry

    lax.fori_loop(0, height_half // 2, weight_three, 0)
    own = filt // n
    for k in range(n):
        for i in range(3):
            g3send[k, i] = acc3[i * filt + k * own : i * filt + (k + 1) * own, :]

    def features(hq, carry):
        y = gathered(dot(a3[...], pair(xp, 2 * hq)), 0, filt, width_half, False)
        for q in range(2):
            put_strided(tc, 2 * hq + q, height_half, y[:, q * width_half : (q + 1) * width_half])
        return carry

    lax.fori_loop(0, height_half // 2, features, 0)
    feat[:, 0] = joined(tc).reshape(filt, height_half, width_half).astype(BF16)
    start_all(g3send, g3recv, s3, r3)

    def volume_row(hc, carry):
        x = xb[:, pl.ds(2 * hc, 4)].reshape((planes + 2) * 4 * chan, width)
        y = dot(b2[...], x)
        for d in range(planes):
            for e in range(2):
                value = gathered(y, (2 * d + e) * 3 * chan, chan, width, True)
                put_strided(tv.at[d], 2 * hc + e, height, value)
        return carry

    halo_arrive(*halos[4])
    lax.fori_loop(0, ready - 1, volume_row, 0)
    g2ag[me] = sum_all(g2send, g2recv, s2, r2)
    lax.fori_loop(ready - 1, ready, volume_row, 0)

    def gather(k, s):
        return pltpu.make_async_remote_copy(
            src_ref=g2ag.at[s],
            dst_ref=g2ag.at[s],
            send_sem=sa.at[k],
            recv_sem=ra.at[s],
            device_id={"gx": k},
            device_id_type=MESH,
        )

    def gather_start(j, carry):
        gather(peer(j), me).start()
        return carry

    lax.fori_loop(1, n, gather_start, 0)

    halo_arrive(*halos[5])
    lax.fori_loop(ready, height_half, volume_row, 0)
    for d in range(planes):
        gvol[:, d] = joined(tv.at[d]).reshape(chan, height, width).astype(BF16)

    total = sum_all(g3send, g3recv, s3, r3)
    for t in range(27):
        g3[t] = total[t % 3, :, chan * (t // 3) : chan * (t // 3 + 1)]

    def gather_wait(j, carry):
        gather(peer(j), peer(j)).wait_recv()
        return carry

    lax.fori_loop(1, n, gather_wait, 0)
    for u in range(units):
        ref, where = place(u)
        ref[where] = g2ag[u // per, u % per * 8 : u % per * 8 + 8]
    for t in range(27):
        i, j = t % 3, t // 3
        if chan * j < 128 * full:
            g2[t] = acc2[i * chan : (i + 1) * chan, chan * j : chan * (j + 1)]
        else:
            g2[t] = tail[:, i * rest : (i + 1) * rest]

    for item in halos:
        halo_sent(*item)
    wait_sends(g2send, g2recv, s2, r2)
    wait_sends(g3send, g3recv, s3, r3)

    def gather_sent(j, carry):
        gather(peer(j), me).wait_send()
        return carry

    lax.fori_loop(1, n, gather_sent, 0)


def local(n, volume, weight_two, weight_three, cotangent):
    chan, planes, height, width = volume.shape
    filt, _, height_half, width_half = cotangent.shape
    taps = 27
    w2 = jnp.transpose(weight_two, (2, 3, 4, 0, 1)).reshape(taps, chan, chan)
    w3 = jnp.transpose(weight_three, (2, 3, 4, 1, 0)).reshape(taps, chan, filt)
    units = 3 * chan // 8 * (9 * chan // 128) + chan // 8
    per = -(-units // n)
    own = filt // n
    wide = (planes + 2) * 4 * chan
    tall = planes * 2 * 3 * chan
    dma = pltpu.SemaphoreType.DMA
    vmem = pl.BlockSpec(memory_space=pltpu.VMEM)
    hbm = pl.BlockSpec(memory_space=pltpu.HBM)
    feat, g3, g2, gvol = pl.pallas_call(
        functools.partial(kernel, n),
        out_shape=(
            jax.ShapeDtypeStruct(cotangent.shape, BF16),
            jax.ShapeDtypeStruct((taps, own, chan), F32),
            jax.ShapeDtypeStruct((taps, chan, chan), F32),
            jax.ShapeDtypeStruct(volume.shape, BF16),
        ),
        in_specs=[hbm] * 4,
        out_specs=(vmem,) * 4,
        scratch_shapes=[
            pltpu.VMEM(volume.shape, BF16),
            pltpu.VMEM(w2.shape, BF16),
            pltpu.VMEM(w3.shape, BF16),
            pltpu.VMEM(cotangent.shape, BF16),
            pltpu.VMEM((planes + 2, height + 2, chan, width), BF16),
            pltpu.VMEM((planes + 2, height + 2, chan, width), BF16),
            pltpu.VMEM((3, height_half + 2, chan, width_half), BF16),
            pltpu.VMEM((3, height_half + 2, filt, width_half), BF16),
            pltpu.VMEM((planes, height, 3 * chan, width), BF16),
            pltpu.VMEM((height_half, 3 * filt, width_half), BF16),
            pltpu.VMEM((planes, width // 128, chan * height, 128), F32),
            pltpu.VMEM((width_half // 128, filt * height_half, 128), F32),
            pltpu.VMEM((height_half, chan, width_half), BF16),
            pltpu.VMEM((tall, wide), BF16),
            pltpu.VMEM((tall, wide), BF16),
            pltpu.VMEM((3 * filt, 9 * chan), BF16),
            pltpu.VMEM((3 * chan, 9 * filt), BF16),
            pltpu.VMEM((3 * chan, 9 * chan), F32),
            pltpu.VMEM((3 * filt, 9 * chan), F32),
            pltpu.VMEM((chan, 128), F32),
            pltpu.VMEM((n, per * 8, 128), F32),
            pltpu.VMEM((n, per * 8, 128), F32),
            pltpu.VMEM((n, per * 8, 128), F32),
            pltpu.VMEM((n, 3, own, 9 * chan), F32),
            pltpu.VMEM((n, 3, own, 9 * chan), F32),
            dma((4,)), dma((12,)), dma((12,)),
            dma((n,)), dma((n,)), dma((n,)), dma((n,)), dma((n,)), dma((n,)),
        ],
        compiler_params=pltpu.CompilerParams(
            collective_id=0, has_side_effects=True, vmem_limit_bytes=67043328
        ),
    )(volume, w2, w3, cotangent)

    def taps_last(grad):
        return jnp.transpose(grad.reshape(3, 3, 3, *grad.shape[1:]), (3, 4, 0, 1, 2))

    return feat, taps_last(g3), taps_last(g2), gvol


def solution(mesh):
    return jax.shard_map(
        functools.partial(local, mesh.shape["gx"]),
        mesh=mesh,
        in_specs=(
            P(None, ("groups", "gx"), None, None),
            P(),
            P(),
            P(None, ("groups", "gx"), None, None),
        ),
        out_specs=(
            P(None, ("groups", "gx"), None, None),
            P(("groups", "gx"), None, None, None, None),
            P("groups", None, None, None, None),
            P(None, ("groups", "gx"), None, None),
        ),
        check_vma=False,
    )
```

```python
import functools

import jax
import jax.numpy as jnp
from jax import lax
from jax.experimental import pallas as pl
from jax.experimental.pallas import tpu as pltpu
from jax.sharding import PartitionSpec as P

F32 = jnp.float32
BF16 = jnp.bfloat16
MESH = pl.DeviceIdType.MESH
NN = (((1,), (0,)), ((), ()))
NT = (((1,), (1,)), ((), ()))


def dot(a, b, dims=NN):
    return lax.dot_general(a, b, dims, preferred_element_type=F32)


def eye(n):
    return (
        lax.broadcasted_iota(jnp.int32, (n, n), 0) == lax.broadcasted_iota(jnp.int32, (n, n), 1)
    ).astype(BF16)


def lane_concat(parts):
    return jnp.concatenate([part.astype(F32) for part in parts], axis=1).astype(BF16)


def lanes(x, period):
    return lax.rem(lax.broadcasted_iota(jnp.int32, x.shape, 1), period)


def before_of(x, period):
    return jnp.where(lanes(x, period) == 0, 0.0, pltpu.roll(x, 1, 1))


def after_of(x, period):
    return jnp.where(lanes(x, period) == period - 1, 0.0, pltpu.roll(x, x.shape[1] - 1, 1))


def gathered(y, at, count, period, flip):
    first, mid, last = (y[at + i * count : at + (i + 1) * count] for i in range(3))
    if flip:
        first, last = last, first
    return before_of(first, period) + mid + after_of(last, period)


def rows_first(ref, value):
    for i in range(ref.shape[0]):
        ref[i] = value[:, 128 * i : 128 * (i + 1)]


def joined(ref):
    return jnp.concatenate([ref[i] for i in range(ref.shape[0])], axis=1)


def strided(ref, start, count, step):
    parts = [ref[i, pl.ds(start, count, stride=step), :] for i in range(ref.shape[0])]
    return jnp.concatenate(parts, axis=1)


def put_strided(ref, start, step, value):
    for i in range(ref.shape[0]):
        ref[i, pl.ds(start, value.shape[0], stride=step), :] = value[:, 128 * i : 128 * (i + 1)]


def zero_rims(stack):
    planes, rows, k, w = stack.shape
    for z in range(planes):
        stack[z, 0] = jnp.zeros((k, w), BF16)
        stack[z, rows - 1] = jnp.zeros((k, w), BF16)


def pair(stack, h):
    k, w = stack.shape[2:]
    rows = stack.shape[0] * 3 * k
    left = stack[:, pl.ds(h, 3)].reshape(rows, w)
    right = stack[:, pl.ds(h + 1, 3)].reshape(rows, w)
    return jnp.concatenate([left, right], axis=1)


def kernel(
    n,
    vol_in, w2_in, w3_in, cot_in,
    feat, g3, g2, gvol,
    vol, w2, w3, cot,
    xs, xb, xp, xc, bs, cs, tv, tc, backs,
    a2, b2, a3, b3, acc2, acc3, tail,
    g2send, g2recv, g2ag, g3send, g3recv,
    load, halo_send, halo_recv, s2, r2, sa, ra, s3, r3,
):
    me = lax.axis_index("gx")
    chan, planes, height, width = vol.shape
    filt, _, height_half, width_half = cot.shape
    barrier = pltpu.get_barrier_semaphore()
    loads = [
        pltpu.make_async_copy(src, dst, load.at[i])
        for i, (src, dst) in enumerate(((cot_in, cot), (vol_in, vol), (w2_in, w2), (w3_in, w3)))
    ]
    for copy in loads:
        copy.start()

    def peer(j):
        return lax.rem(me + j, n)

    def greet(j, carry):
        pl.semaphore_signal(barrier, inc=1, device_id={"gx": peer(j)}, device_id_type=MESH)
        return carry

    lax.fori_loop(1, n, greet, 0)

    def halo(slot, stack, part, parts, up):
        index = 2 * slot + (0 if up else 1)
        last = stack.shape[0] - 1
        count = (stack.shape[1] - 2) // parts
        rows = pl.ds(1 + part * count, count)
        return pltpu.make_async_remote_copy(
            src_ref=stack.at[last - 1 if up else 1, rows],
            dst_ref=stack.at[0 if up else last, rows],
            send_sem=halo_send.at[index],
            recv_sem=halo_recv.at[index],
            device_id={"gx": lax.rem(me + (1 if up else n - 1), n)},
            device_id_type=MESH,
        )

    def halo_start(*item):
        @pl.when(me < n - 1)
        def _():
            halo(*item, True).start()

        @pl.when(me > 0)
        def _():
            halo(*item, False).start()

    def halo_arrive(*item):
        @pl.when(me > 0)
        def _():
            halo(*item, True).wait_recv()

        @pl.when(me < n - 1)
        def _():
            halo(*item, False).wait_recv()

    def halo_sent(*item):
        @pl.when(me < n - 1)
        def _():
            halo(*item, True).wait_send()

        @pl.when(me > 0)
        def _():
            halo(*item, False).wait_send()

    halos = (
        (0, xs, 0, 2), (1, xs, 1, 2), (2, xc, 0, 1), (3, xp, 0, 1), (4, xb, 0, 2), (5, xb, 1, 2)
    )

    loads[0].wait()
    rows_first(tc, cot[:, 0].astype(F32).reshape(filt * height_half, width_half))

    def cot_row(h, carry):
        x = strided(tc, h, filt, height_half)
        xc[1, h + 1] = x.astype(BF16)
        cs[h, 0:filt] = after_of(x, width_half).astype(BF16)
        cs[h, filt : 2 * filt] = x.astype(BF16)
        cs[h, 2 * filt : 3 * filt] = before_of(x, width_half).astype(BF16)
        return carry

    lax.fori_loop(0, height_half, cot_row, 0)
    loads[1].wait()
    for d in range(planes):
        rows_first(tv.at[d], vol[:, d].astype(F32).reshape(chan * height, width))

        def vol_row(h, carry, d=d):
            xs[d + 1, h + 1] = strided(tv.at[d], h, chan, height).astype(BF16)
            return carry

        lax.fori_loop(0, height, vol_row, 0)
    for stack in (xs, xb, xp, xc):
        zero_rims(stack)
    pl.semaphore_wait(barrier, n - 1)
    halo_start(*halos[2])
    halo_start(*halos[0])
    halo_start(*halos[1])

    @pl.when(me == 0)
    def _():
        for stack in (xs, xb, xp, xc):
            stack[0] = jnp.zeros(stack.shape[1:], BF16)

    @pl.when(me == n - 1)
    def _():
        for stack in (xs, xb, xp, xc):
            stack[stack.shape[0] - 1] = jnp.zeros(stack.shape[1:], BF16)

    loads[2].wait()
    loads[3].wait()
    hole = jnp.zeros((chan, chan), BF16)
    gap = jnp.zeros((chan, 4 * chan), BF16)
    for e in range(2):
        for i in range(3):
            ahead, back = [], []
            for dz in range(3):
                for y in range(4):
                    inside = 0 <= y - e <= 2
                    ahead.append(w2[9 * dz + 3 * (y - e) + i] if inside else hole)
                    back.append(w2[9 * (2 - dz) + 3 * (2 - y + e) + i] if inside else hole)
            group = lane_concat(ahead)
            flipped = dot(eye(chan), jnp.concatenate(back, axis=0), NT).astype(BF16)
            for d in range(planes):
                rows = slice(((2 * d + e) * 3 + i) * chan, ((2 * d + e) * 3 + i + 1) * chan)
                for big, part in ((a2, group), (b2, flipped)):
                    line = [gap] * d + [part] + [gap] * (planes - 1 - d)
                    big[rows, :] = jnp.concatenate(line, axis=1)
    for i in range(3):
        taps_in = [w3[3 * t + i] for t in range(9)]
        taps_out = [w3[3 * (8 - t) + i] for t in range(9)]
        b3[i * chan : (i + 1) * chan, :] = lane_concat(taps_out)
        a3[i * filt : (i + 1) * filt, :] = dot(
            eye(filt), jnp.concatenate(taps_in, axis=0), NT
        ).astype(BF16)

    fine = lax.broadcasted_iota(jnp.int32, (width, width_half), 0)
    coarse = lax.broadcasted_iota(jnp.int32, (width, width_half), 1)
    pool = ((fine == 2 * coarse) | (fine == 2 * coarse + 1)).astype(BF16)

    halo_arrive(*halos[2])

    def coarse_back(hq, carry):
        y = dot(b3[...], pair(xc, 2 * hq))
        value = gathered(y, 0, chan, width_half, True).astype(BF16)
        for q in range(2):
            backs[2 * hq + q] = value[:, q * width_half : (q + 1) * width_half]
        return carry

    lax.fori_loop(0, height_half // 2, coarse_back, 0)

    def forward(hc, carry):
        x = xs[:, pl.ds(2 * hc, 4)].reshape((planes + 2) * 4 * chan, width)
        y = dot(a2[...], x)
        spread = dot(backs[hc], pool, NT) * 0.125
        total = jnp.zeros((chan, width), F32)
        for d in range(planes):
            for e in range(2):
                h = 2 * hc + e
                before = gathered(y, (2 * d + e) * 3 * chan, chan, width, False)
                sigma = jax.nn.sigmoid(before)
                total = total + (before * sigma).astype(BF16).astype(F32)
                value = (spread * (sigma * (1.0 + before * (1.0 - sigma)))).astype(BF16)
                wide = value.astype(F32)
                xb[d + 1, h + 1] = value
                bs[d, h, 0:chan] = after_of(wide, width).astype(BF16)
                bs[d, h, chan : 2 * chan] = value
                bs[d, h, 2 * chan : 3 * chan] = before_of(wide, width).astype(BF16)
        high = total.astype(BF16)
        low = (total - high.astype(F32)).astype(BF16)
        xp[1, hc + 1] = ((dot(high, pool) + dot(low, pool)) * 0.125).astype(BF16)
        return carry

    ready = height_half // 2 - 1
    halo_arrive(*halos[0])
    lax.fori_loop(0, ready, forward, 0)
    halo_arrive(*halos[1])
    lax.fori_loop(ready, height_half, forward, 0)

    def weight_two(h, total):
        for d in range(planes):
            x = xs[d : d + 3, pl.ds(h, 3)].reshape(9 * chan, width)
            total = total + dot(bs[d, h], x, NT)
        return total

    acc2[...] = weight_two(0, jnp.zeros(acc2.shape, F32))
    halo_start(*halos[3])
    halo_start(*halos[4])
    halo_start(*halos[5])

    def more_two(h, carry):
        acc2[...] = weight_two(h, acc2[...])
        return carry

    lax.fori_loop(1, height, more_two, 0)

    full = acc2.shape[1] // 128
    rest = acc2.shape[1] - 128 * full
    groups = acc2.shape[0] // 8
    units = full * groups + chan // 8
    per = g2send.shape[1] // 8
    tail[...] = jnp.concatenate(
        [acc2[i * chan : (i + 1) * chan, 128 * full :] for i in range(3)]
        + [jnp.zeros((chan, 128 - 3 * rest), F32)],
        axis=1,
    )

    def place(u):
        j, r = u // groups, u % groups
        if j == full:
            return tail, (slice(8 * r, 8 * r + 8), slice(0, 128))
        return acc2, (slice(8 * r, 8 * r + 8), slice(128 * j, 128 * j + 128))

    for u in range(n * per):
        at = (u // per, slice(u % per * 8, u % per * 8 + 8))
        if u < units:
            ref, where = place(u)
            g2send[at] = ref[where]
        else:
            g2send[at] = jnp.zeros((8, 128), F32)

    def scatter(send, recv, ssem, rsem, k, s):
        return pltpu.make_async_remote_copy(
            src_ref=send.at[k],
            dst_ref=recv.at[s],
            send_sem=ssem.at[k],
            recv_sem=rsem.at[s],
            device_id={"gx": k},
            device_id_type=MESH,
        )

    def start_all(send, recv, ssem, rsem):
        def one(j, carry):
            scatter(send, recv, ssem, rsem, peer(j), me).start()
            return carry

        lax.fori_loop(1, n, one, 0)

    def wait_sends(send, recv, ssem, rsem):
        def one(j, carry):
            scatter(send, recv, ssem, rsem, peer(j), me).wait_send()
            return carry

        lax.fori_loop(1, n, one, 0)

    def sum_all(send, recv, ssem, rsem):
        def one(j, total):
            s = peer(j)
            scatter(send, recv, ssem, rsem, s, s).wait_recv()
            return total + recv[s]

        return lax.fori_loop(1, n, one, send[me])

    halo_arrive(*halos[3])
    start_all(g2send, g2recv, s2, r2)

    acc3[...] = jnp.zeros(acc3.shape, F32)

    def weight_three(hq, carry):
        upstream = jnp.concatenate([cs[2 * hq], cs[2 * hq + 1]], axis=1)
        acc3[...] += dot(upstream, pair(xp, 2 * hq), NT)
        return carry

    lax.fori_loop(0, height_half // 2, weight_three, 0)
    own = filt // n
    for k in range(n):
        for i in range(3):
            g3send[k, i] = acc3[i * filt + k * own : i * filt + (k + 1) * own, :]

    def features(hq, carry):
        y = gathered(dot(a3[...], pair(xp, 2 * hq)), 0, filt, width_half, False)
        for q in range(2):
            put_strided(tc, 2 * hq + q, height_half, y[:, q * width_half : (q + 1) * width_half])
        return carry

    lax.fori_loop(0, height_half // 2, features, 0)
    cot[:, 0] = joined(tc).reshape(filt, height_half, width_half).astype(BF16)
    store_feat = pltpu.make_async_copy(cot, feat, load.at[0])
    store_feat.start()
    start_all(g3send, g3recv, s3, r3)

    def volume_row(hc, carry):
        x = xb[:, pl.ds(2 * hc, 4)].reshape((planes + 2) * 4 * chan, width)
        y = dot(b2[...], x)
        for d in range(planes):
            for e in range(2):
                value = gathered(y, (2 * d + e) * 3 * chan, chan, width, True)
                put_strided(tv.at[d], 2 * hc + e, height, value)
        return carry

    halo_arrive(*halos[4])
    lax.fori_loop(0, ready - 1, volume_row, 0)
    g2ag[me] = sum_all(g2send, g2recv, s2, r2)
    lax.fori_loop(ready - 1, ready, volume_row, 0)

    def gather(k, s):
        return pltpu.make_async_remote_copy(
            src_ref=g2ag.at[s],
            dst_ref=g2ag.at[s],
            send_sem=sa.at[k],
            recv_sem=ra.at[s],
            device_id={"gx": k},
            device_id_type=MESH,
        )

    def gather_start(j, carry):
        gather(peer(j), me).start()
        return carry

    lax.fori_loop(1, n, gather_start, 0)

    halo_arrive(*halos[5])
    lax.fori_loop(ready, height_half, volume_row, 0)
    for d in range(planes):
        vol[:, d] = joined(tv.at[d]).reshape(chan, height, width).astype(BF16)
    store_vol = pltpu.make_async_copy(vol, gvol, load.at[1])
    store_vol.start()

    total = sum_all(g3send, g3recv, s3, r3)
    for t in range(27):
        g3[t] = total[t % 3, :, chan * (t // 3) : chan * (t // 3 + 1)]

    def gather_wait(j, carry):
        gather(peer(j), peer(j)).wait_recv()
        return carry

    lax.fori_loop(1, n, gather_wait, 0)
    for u in range(units):
        ref, where = place(u)
        ref[where] = g2ag[u // per, u % per * 8 : u % per * 8 + 8]
    for t in range(27):
        i, j = t % 3, t // 3
        if chan * j < 128 * full:
            g2[t] = acc2[i * chan : (i + 1) * chan, chan * j : chan * (j + 1)]
        else:
            g2[t] = tail[:, i * rest : (i + 1) * rest]

    store_feat.wait()
    store_vol.wait()
    for item in halos:
        halo_sent(*item)
    wait_sends(g2send, g2recv, s2, r2)
    wait_sends(g3send, g3recv, s3, r3)

    def gather_sent(j, carry):
        gather(peer(j), me).wait_send()
        return carry

    lax.fori_loop(1, n, gather_sent, 0)


def local(n, volume, weight_two, weight_three, cotangent):
    chan, planes, height, width = volume.shape
    filt, _, height_half, width_half = cotangent.shape
    taps = 27
    w2 = jnp.transpose(weight_two, (2, 3, 4, 0, 1)).reshape(taps, chan, chan)
    w3 = jnp.transpose(weight_three, (2, 3, 4, 1, 0)).reshape(taps, chan, filt)
    units = 3 * chan // 8 * (9 * chan // 128) + chan // 8
    per = -(-units // n)
    own = filt // n
    wide = (planes + 2) * 4 * chan
    tall = planes * 2 * 3 * chan
    dma = pltpu.SemaphoreType.DMA
    vmem = pl.BlockSpec(memory_space=pltpu.VMEM)
    hbm = pl.BlockSpec(memory_space=pltpu.HBM)
    feat, g3, g2, gvol = pl.pallas_call(
        functools.partial(kernel, n),
        out_shape=(
            jax.ShapeDtypeStruct(cotangent.shape, BF16),
            jax.ShapeDtypeStruct((taps, own, chan), F32),
            jax.ShapeDtypeStruct((taps, chan, chan), F32),
            jax.ShapeDtypeStruct(volume.shape, BF16),
        ),
        in_specs=[hbm] * 4,
        out_specs=(hbm, vmem, vmem, hbm),
        scratch_shapes=[
            pltpu.VMEM(volume.shape, BF16),
            pltpu.VMEM(w2.shape, BF16),
            pltpu.VMEM(w3.shape, BF16),
            pltpu.VMEM(cotangent.shape, BF16),
            pltpu.VMEM((planes + 2, height + 2, chan, width), BF16),
            pltpu.VMEM((planes + 2, height + 2, chan, width), BF16),
            pltpu.VMEM((3, height_half + 2, chan, width_half), BF16),
            pltpu.VMEM((3, height_half + 2, filt, width_half), BF16),
            pltpu.VMEM((planes, height, 3 * chan, width), BF16),
            pltpu.VMEM((height_half, 3 * filt, width_half), BF16),
            pltpu.VMEM((planes, width // 128, chan * height, 128), F32),
            pltpu.VMEM((width_half // 128, filt * height_half, 128), F32),
            pltpu.VMEM((height_half, chan, width_half), BF16),
            pltpu.VMEM((tall, wide), BF16),
            pltpu.VMEM((tall, wide), BF16),
            pltpu.VMEM((3 * filt, 9 * chan), BF16),
            pltpu.VMEM((3 * chan, 9 * filt), BF16),
            pltpu.VMEM((3 * chan, 9 * chan), F32),
            pltpu.VMEM((3 * filt, 9 * chan), F32),
            pltpu.VMEM((chan, 128), F32),
            pltpu.VMEM((n, per * 8, 128), F32),
            pltpu.VMEM((n, per * 8, 128), F32),
            pltpu.VMEM((n, per * 8, 128), F32),
            pltpu.VMEM((n, 3, own, 9 * chan), F32),
            pltpu.VMEM((n, 3, own, 9 * chan), F32),
            dma((4,)), dma((12,)), dma((12,)),
            dma((n,)), dma((n,)), dma((n,)), dma((n,)), dma((n,)), dma((n,)),
        ],
        compiler_params=pltpu.CompilerParams(
            collective_id=0, has_side_effects=True, vmem_limit_bytes=67043328
        ),
    )(volume, w2, w3, cotangent)

    def taps_last(grad):
        return jnp.transpose(grad.reshape(3, 3, 3, *grad.shape[1:]), (3, 4, 0, 1, 2))

    return feat, taps_last(g3), taps_last(g2), gvol


def solution(mesh):
    return jax.shard_map(
        functools.partial(local, mesh.shape["gx"]),
        mesh=mesh,
        in_specs=(
            P(None, ("groups", "gx"), None, None),
            P(),
            P(),
            P(None, ("groups", "gx"), None, None),
        ),
        out_specs=(
            P(None, ("groups", "gx"), None, None),
            P(("groups", "gx"), None, None, None, None),
            P("groups", None, None, None, None),
            P(None, ("groups", "gx"), None, None),
        ),
        check_vma=False,
    )
```
